32 devices in a mesh: ctx: 8 (over y, x, core), head: 4 (over z).
Axes of the slice: x: 2, y: 2, z: 4, core: 2. Of those that a mesh axis runs over, the one named last changes fastest.
Arguments:
- tokens: bfloat16 [8192, 2048], P('ctx', 'head'), may hold values from -6 to 6
- w_query: bfloat16 [2048, 2048], P(None, 'head'), may hold values from -0.125 to 0.125
- w_value: bfloat16 [2048, 2048], P(None, 'head'), may hold values from -0.125 to 0.125
- w_out: bfloat16 [2048, 2048], P('head'), may hold values from -1.5 to 1.5
- doc_lengths: int32 [2], replicated, may hold values from 512 to 4096, as said below
Outputs:
- layer_out: bfloat16 [8192, 2048], P('ctx', 'head')
The draws below stay inside these ranges and needn't reach their ends.
Inputs may be any that keep to these rules, and one draw needn't show every extreme that they name: `doc_lengths`: one of the two documents, drawn from the seed, has the full length 4096; the other has at least 512 valid tokens.
All inputs are finite; a program needn't handle non-finite values.
Results may differ from the reference program's by a relative error of at most 0.02.
Values may be sent and summed in bfloat16 or wider, within the bound.
A program may use at most 64 MiB of HBM per device.

```python
import jax
import jax.numpy as jnp
from jax import lax

D = 2048
H = 16
HD = 128
TOK_DEV = 1024
DOC_LEN = 4096
TOKENS = 8192


def draw_lengths(key, part):
    lowest = max(DOC_LEN // 8, 2)
    picked = jax.random.randint(jax.random.fold_in(key, 11), (2,), lowest, DOC_LEN + 1)
    full_doc = jax.random.randint(jax.random.fold_in(key, 12), (), 0, 2)
    return jnp.where(jnp.arange(2) == full_doc, DOC_LEN, picked).astype(jnp.int32)


def draw_doc_lengths(key, part):
    return draw_lengths(key, part)


def with_spikes(entries, stream_key, source, target, blocks, factor):
    def block_of(dim):
        return (jnp.arange(entries.shape[dim]) // (entries.shape[dim] // blocks)).reshape((-1,) + (1,) * (entries.ndim - 1 - dim))

    near = jax.random.permutation(stream_key, blocks)[block_of(target)]
    far = (block_of(target) + blocks // 2) % blocks
    return jnp.where((block_of(source) == near) | (block_of(source) == far), factor * entries, entries)


def steps_of(key, extent, cuts, smallest, high):
    loudness, own = 1.0, jax.random.fold_in(key, 6)
    for dim, shards_of in cuts:
        draws = jnp.exp(jax.random.uniform(jax.random.fold_in(own, dim), (shards_of,), jnp.float32, smallest / len(cuts), high / len(cuts)))
        loudness = loudness * jnp.repeat(draws, extent[dim] // shards_of).reshape([-1 if axis == dim else 1 for axis in range(len(extent))])
    return loudness


def gaussian(rng, dims, spread, bound, shards=(), kind=jnp.bfloat16):
    values = jax.random.normal(rng, dims, jnp.float32) * spread
    if len(shards) > 0:
        values = steps_of(rng, dims, shards, -0.22, 0.18) * values
    return jnp.clip(values, min=-bound, max=bound).astype(kind)


def noise_with(rng, dims, width, reach, split, heavy, kind=jnp.bfloat16):
    entries = width * jax.random.normal(rng, dims, jnp.float32)
    if split:
        entries = entries * steps_of(rng, dims, split, -0.22, 0.18)
    return jnp.clip(with_spikes(entries, jax.random.fold_in(rng, 3), *heavy), -reach, reach).astype(kind)


def setup_inputs(seed: int = 0) -> dict:
    splits = jax.random.split(jax.random.key(seed), 6)
    tokens = gaussian(splits[0], (TOKENS, D), 1.0, 6.0, ((0, 8), (1, 4)))
    w_query = gaussian(splits[1], (D, H * HD), D ** -0.5, 0.125, ((1, 4),))
    w_value = gaussian(splits[2], (D, H * HD), D ** -0.5, 0.125, ((1, 4),))
    w_out = noise_with(splits[3], (H * HD, D), (HD // 4) ** -0.5, 1.5, ((0, 4),), (0, 1, 4, 2.0))
    doc_lengths = draw_doc_lengths(jax.random.fold_in(splits[5], 71), 0)
    return {"tokens": tokens, "w_query": w_query, "w_value": w_value, "w_out": w_out, "doc_lengths": doc_lengths}


score_bound = 24.0

def reference(tokens, w_query, w_value, w_out, doc_lengths):
    projected = jnp.dot(tokens, w_query, preferred_element_type=jnp.float32).reshape(TOKENS, H, HD)
    unit_rows = projected * lax.rsqrt(lax.optimization_barrier(jnp.sum(projected * projected, axis=-1, keepdims=True)) + 1e-06)
    unit_rows = lax.optimization_barrier(unit_rows.astype(jnp.bfloat16)).astype(jnp.float32)
    value_rows = jnp.dot(tokens, w_value, preferred_element_type=jnp.float32).astype(jnp.bfloat16)
    value_rows = lax.optimization_barrier(value_rows).astype(jnp.float32).reshape(TOKENS, H, HD)
    position = jnp.arange(TOKENS, dtype=jnp.int32)
    doc_index = position // DOC_LEN
    limit = jnp.where(doc_index == 0, doc_lengths[0], doc_lengths[1])
    valid_rows = (position - doc_index * DOC_LEN < limit).astype(jnp.float32)
    per_doc = DOC_LEN // TOK_DEV

    def one_block(block_index):
        start = (block_index * TOK_DEV).astype(jnp.int32)
        query_rows = lax.dynamic_slice_in_dim(unit_rows, start, TOK_DEV, 0)
        query_valid = lax.dynamic_slice_in_dim(valid_rows, start, TOK_DEV, 0)
        query_position = start + jnp.arange(TOK_DEV, dtype=jnp.int32)
        doc_start = (start // DOC_LEN * DOC_LEN).astype(jnp.int32)

        def add_keys(key_block, totals):
            numer, denom = totals
            key_start = (doc_start + key_block * TOK_DEV).astype(jnp.int32)
            key_rows = lax.dynamic_slice_in_dim(unit_rows, key_start, TOK_DEV, 0)
            key_values = lax.dynamic_slice_in_dim(value_rows, key_start, TOK_DEV, 0)
            key_valid = lax.dynamic_slice_in_dim(valid_rows, key_start, TOK_DEV, 0)
            key_position = key_start + jnp.arange(TOK_DEV, dtype=jnp.int32)
            distinct = (query_position[:, None] != key_position[None, :]).astype(jnp.float32)
            pair_mask = query_valid[:, None] * key_valid[None, :] * distinct
            scores = jnp.einsum('qhd,khd->hqk', query_rows, key_rows) * score_bound
            tile = jnp.exp(scores - score_bound) * pair_mask[None]
            denom = denom + lax.optimization_barrier(jnp.sum(tile, axis=2))
            rounded = lax.optimization_barrier(tile.astype(jnp.bfloat16)).astype(jnp.float32)
            numer = numer + jnp.einsum('hqk,khd->qhd', rounded, key_values)
            return (numer, denom)
        start_totals = (jnp.zeros((TOK_DEV, H, HD), jnp.float32), jnp.zeros((H, TOK_DEV), jnp.float32))
        numer, denom = lax.fori_loop(0, per_doc, add_keys, start_totals)
        attended = numer / (denom.T[:, :, None] + (1.0 - query_valid)[:, None, None])
        return attended.astype(jnp.bfloat16)
    blocks = lax.map(one_block, jnp.arange(TOKENS // TOK_DEV, dtype=jnp.int32))
    attended = blocks.reshape(TOKENS, H * HD)
    return jnp.dot(attended, w_out, preferred_element_type=jnp.float32).astype(jnp.bfloat16)
```

```python
import functools
import math

import jax
import jax.numpy as jnp
from jax import lax
from jax.experimental import pallas as pl
from jax.experimental.pallas import tpu as pltpu
from jax.sharding import PartitionSpec as P

HD = 128
SCORE_BOUND = 24.0
EXP2_SCALE = SCORE_BOUND * math.log2(math.e)
GATHER_CHUNKS = 8
QUERY_CHUNKS = 4
MESH = pl.DeviceIdType.MESH


def layer_kernel(
    n, g, tok_hbm, wq_hbm, wv_hbm, wo_hbm, lengths, out_ref,
    tok, w, wo, q, kv, ones, att, from_low, from_high, outgoing, own_sum,
    load_sem, up_send, down_send, tok_recv, kv_send, kv_pass, kv_recv,
    sum_send, low_recv, high_recv,
):
    rows, wide = tok_hbm.shape
    heads = wide // HD
    half = g // 2
    gather_chunks, query_chunks = GATHER_CHUNKS, QUERY_CHUNKS
    step_rows = rows // gather_chunks
    query_rows = rows // query_chunks
    k = lax.axis_index("head")
    ctx = lax.axis_index("ctx")
    doc = ctx // g
    base = doc * g
    j = ctx - base
    partner = j + 1 - 2 * lax.rem(j, 2)

    loads = [
        pltpu.make_async_copy(tok_hbm, tok.at[k], load_sem.at[0]),
        pltpu.make_async_copy(wq_hbm, w.at[:, pl.ds(0, wide)], load_sem.at[1]),
        pltpu.make_async_copy(wv_hbm, w.at[:, pl.ds(wide, wide)], load_sem.at[2]),
        pltpu.make_async_copy(wo_hbm, wo, load_sem.at[3]),
    ]
    for load in loads:
        load.start()

    barrier = pltpu.get_barrier_semaphore()

    def greet(where):
        pl.semaphore_signal(barrier, inc=1, device_id=where, device_id_type=MESH)

    @pl.when(k > 0)
    def _():
        greet({"head": k - 1})

    @pl.when(k < n - 1)
    def _():
        greet({"head": k + 1})

    greet({"ctx": base + partner})
    for m in range(1, half):
        greet({"ctx": base + lax.rem(j + 2 * m, g)})
    pl.semaphore_wait(
        barrier, jnp.where(k > 0, 1, 0) + jnp.where(k < n - 1, 1, 0) + half
    )

    limit = jnp.where(doc == 0, lengths[0], lengths[1])

    def valid_rows(first, count):
        position = first + lax.broadcasted_iota(jnp.int32, (count, HD), 0)
        return jnp.where(position < limit, 1.0, 0.0)

    def chunk(c):
        return pl.ds(pl.multiple_of(c * step_rows, step_rows), step_rows)

    def tok_copy(source, c, to, sends):
        piece = tok.at[source, chunk(c)]
        return pltpu.make_async_remote_copy(
            src_ref=piece, dst_ref=piece, send_sem=sends.at[source, c],
            recv_sem=tok_recv.at[source, c], device_id={"head": to}, device_id_type=MESH,
        )

    def send_tok(source, c, up):
        if up:
            @pl.when(k < n - 1)
            def _():
                tok_copy(source, c, k + 1, up_send).start()
        else:
            @pl.when(k > 0)
            def _():
                tok_copy(source, c, k - 1, down_send).start()

    def arrive(source, c, up):
        tok_copy(source, c, k, up_send).wait_recv()
        send_tok(source, c, up)

    def kv_copy(slot, c, to, sem):
        piece = kv.at[slot, chunk(c)]
        return pltpu.make_async_remote_copy(
            src_ref=piece, dst_ref=piece, send_sem=sem, recv_sem=kv_recv.at[slot, c],
            device_id={"ctx": base + to}, device_id_type=MESH,
        )

    def behind(m):
        return lax.rem(j + g - 2 * m, g)

    def pass_on(c):
        for m in range(1, half):
            slot = behind(m)
            kv_copy(slot, c, partner, kv_pass.at[m, c]).wait_recv()
            kv_copy(slot, c, partner, kv_pass.at[m, c]).start()

    loads[0].wait()
    send_tok(k, 0, True)
    send_tok(k, 0, False)
    ones[...] = jnp.concatenate(
        [valid_rows(block * rows, rows) for block in range(g)], axis=0
    ).astype(jnp.bfloat16)
    loads[1].wait()
    loads[2].wait()

    def gather_step(c, carry):
        for distance in range(1, n):
            @pl.when(k - distance >= 0)
            def _():
                arrive(k - distance, c, True)

            @pl.when(k + distance < n)
            def _():
                arrive(k + distance, c, False)

        @pl.when(c + 1 < gather_chunks)
        def _():
            send_tok(k, c + 1, True)
            send_tok(k, c + 1, False)

        total = jnp.dot(tok[0, chunk(c)], w[0:wide], preferred_element_type=jnp.float32)
        for s in range(1, n):
            total += jnp.dot(
                tok[s, chunk(c)], w[s * wide:(s + 1) * wide],
                preferred_element_type=jnp.float32,
            )
        valid = valid_rows(j * rows + c * step_rows, step_rows)
        for h in range(heads):
            columns = slice(h * HD, (h + 1) * HD)
            part = total[:, columns]
            unit = part * lax.rsqrt(jnp.sum(part * part, axis=1, keepdims=True) + 1e-06)
            kv[j, chunk(c), columns] = unit.astype(jnp.bfloat16)
            q[chunk(c), columns] = (unit * EXP2_SCALE).astype(jnp.bfloat16)
            shifted = slice(wide + h * HD, wide + (h + 1) * HD)
            kv[j, chunk(c), shifted] = (total[:, shifted] * valid).astype(jnp.bfloat16)
        for m in range(1, half):
            kv_copy(j, c, lax.rem(j + 2 * m, g), kv_send.at[m, c]).start()
        kv_copy(j, c, partner, kv_send.at[0, c]).start()

        @pl.when(c > 0)
        def _():
            pass_on(c - 1)

        return carry

    lax.fori_loop(0, gather_chunks, gather_step, 0)
    pass_on(gather_chunks - 1)
    loads[3].wait()

    def gather_end(c, carry):
        kv_copy(partner, c, partner, kv_send.at[0, c]).wait_recv()
        for m in range(1, half):
            slot = lax.rem(partner + g - 2 * m, g)
            kv_copy(slot, c, partner, kv_pass.at[m, c]).wait_recv()
        return carry

    lax.fori_loop(0, gather_chunks, gather_end, 0)

    def sum_copy(c, d, to, landing, recv):
        return pltpu.make_async_remote_copy(
            src_ref=outgoing.at[c, d], dst_ref=landing.at[c, d], send_sem=sum_send.at[c, d],
            recv_sem=recv.at[c, d], device_id={"head": to}, device_id_type=MESH,
        )

    def query_chunk(c):
        return pl.ds(pl.multiple_of(c * query_rows, query_rows), query_rows)

    def share(d):
        columns = pl.ds(pl.multiple_of(d * wide, HD), wide)
        return jnp.dot(att[...], wo[:, columns], preferred_element_type=jnp.float32)

    def query_step(c, carry):
        own = c * query_rows
        valid = valid_rows(j * rows + own, query_rows)
        row = lax.broadcasted_iota(jnp.int32, (query_rows, rows), 0) + own
        column = lax.broadcasted_iota(jnp.int32, (query_rows, rows), 1)
        for h in range(heads):
            columns = slice(h * HD, (h + 1) * HD)
            shifted = slice(wide + h * HD, wide + (h + 1) * HD)
            queries = q[query_chunk(c), columns]
            total = None
            for b in range(g):
                block = lax.rem(j + b, g)
                scores = lax.dot_general(
                    queries, kv[block, :, columns], (((1,), (1,)), ((), ())),
                    preferred_element_type=jnp.float32,
                )
                weights = jnp.exp2(scores)
                if b == 0:
                    weights = jnp.where(row != column, weights, 0.0)
                block_rows = pl.ds(pl.multiple_of(block * rows, rows), rows)
                values = jnp.concatenate(
                    [kv[block, :, shifted], ones[block_rows]], axis=1
                )
                term = jnp.dot(
                    weights.astype(jnp.bfloat16), values, preferred_element_type=jnp.float32
                )
                total = term if total is None else total + term
            result = valid * total[:, :HD] / (total[:, HD:] + (1.0 - valid))
            att[:, columns] = result.astype(jnp.bfloat16)

        def emit(d, to, waits, landing, recv):
            @pl.when(waits)
            def _():
                sum_copy(c, d, k, landing, recv).wait_recv()
                outgoing[c, d] = (share(d) + landing[c, d].astype(jnp.float32)).astype(
                    jnp.bfloat16
                )

            @pl.when(jnp.logical_not(waits))
            def _():
                outgoing[c, d] = share(d).astype(jnp.bfloat16)

            sum_copy(c, d, to, landing, recv).start()

        for off in range(n - 1, 0, -1):
            @pl.when(k + off < n)
            def _():
                emit(k + off, k + 1, k > 0, from_low, low_recv)

            @pl.when(k - off >= 0)
            def _():
                emit(k - off, k - 1, k < n - 1, from_high, high_recv)

        own_sum[query_chunk(c)] = share(k)
        return carry

    lax.fori_loop(0, query_chunks, query_step, 0)

    def finish(c, carry):
        @pl.when(k > 0)
        def _():
            sum_copy(c, k, k, from_low, low_recv).wait_recv()
            own_sum[query_chunk(c)] += from_low[c, k].astype(jnp.float32)

        @pl.when(k < n - 1)
        def _():
            sum_copy(c, k, k, from_high, high_recv).wait_recv()
            own_sum[query_chunk(c)] += from_high[c, k].astype(jnp.float32)

        out_ref[query_chunk(c)] = own_sum[query_chunk(c)].astype(out_ref.dtype)
        return carry

    lax.fori_loop(0, query_chunks, finish, 0)

    def drain_gather(c, carry):
        for s in range(n):
            @pl.when(jnp.logical_and(s <= k, k < n - 1))
            def _():
                tok_copy(s, c, k + 1, up_send).wait_send()

            @pl.when(jnp.logical_and(s >= k, k > 0))
            def _():
                tok_copy(s, c, k - 1, down_send).wait_send()

        kv_copy(j, c, partner, kv_send.at[0, c]).wait_send()
        for m in range(1, half):
            kv_copy(j, c, partner, kv_send.at[m, c]).wait_send()
            kv_copy(behind(m), c, partner, kv_pass.at[m, c]).wait_send()
        return carry

    lax.fori_loop(0, gather_chunks, drain_gather, 0)

    def drain_sums(c, carry):
        for d in range(n):
            @pl.when(d > k)
            def _():
                sum_copy(c, d, k + 1, from_low, low_recv).wait_send()

            @pl.when(d < k)
            def _():
                sum_copy(c, d, k - 1, from_high, high_recv).wait_send()

        return carry

    lax.fori_loop(0, query_chunks, drain_sums, 0)


def per_device(tokens, w_query, w_value, w_out, doc_lengths):
    n = lax.axis_size("head")
    g = lax.axis_size("ctx") // 2
    rows, wide = tokens.shape
    depth = w_query.shape[0]
    query_rows = rows // QUERY_CHUNKS
    bf16, f32 = jnp.bfloat16, jnp.float32
    dma = pltpu.SemaphoreType.DMA
    any_space = pl.BlockSpec(memory_space=pl.ANY)
    pieces = (QUERY_CHUNKS, n, query_rows, wide)
    return pl.pallas_call(
        functools.partial(layer_kernel, n, g),
        out_shape=jax.ShapeDtypeStruct((rows, wide), bf16),
        in_specs=[any_space] * 4 + [pl.BlockSpec(memory_space=pltpu.SMEM)],
        out_specs=pl.BlockSpec(memory_space=pltpu.VMEM),
        scratch_shapes=[
            pltpu.VMEM((n, rows, wide), bf16),
            pltpu.VMEM((depth, 2 * wide), bf16),
            pltpu.VMEM(w_out.shape, bf16),
            pltpu.VMEM((rows, wide), bf16),
            pltpu.VMEM((g, rows, 2 * wide), bf16),
            pltpu.VMEM((g * rows, HD), bf16),
            pltpu.VMEM((query_rows, wide), bf16),
            pltpu.VMEM(pieces, bf16),
            pltpu.VMEM(pieces, bf16),
            pltpu.VMEM(pieces, bf16),
            pltpu.VMEM((rows, wide), f32),
            dma((4,)),
            dma((n, GATHER_CHUNKS)),
            dma((n, GATHER_CHUNKS)),
            dma((n, GATHER_CHUNKS)),
            dma((g // 2, GATHER_CHUNKS)),
            dma((g // 2, GATHER_CHUNKS)),
            dma((g, GATHER_CHUNKS)),
            dma((QUERY_CHUNKS, n)),
            dma((QUERY_CHUNKS, n)),
            dma((QUERY_CHUNKS, n)),
        ],
        compiler_params=pltpu.CompilerParams(
            collective_id=0, has_side_effects=True, vmem_limit_bytes=60 * 1024 * 1024
        ),
    )(tokens, w_query, w_value, w_out, doc_lengths)


def solution(mesh):
    return jax.shard_map(
        per_device,
        mesh=mesh,
        in_specs=(P("ctx", "head"), P(None, "head"), P(None, "head"), P("head", None), P()),
        out_specs=P("ctx", "head"),
        check_vma=False,
    )
```

```python
import functools
import math

import jax
import jax.numpy as jnp
from jax import lax
from jax.experimental import pallas as pl
from jax.experimental.pallas import tpu as pltpu
from jax.sharding import PartitionSpec as P

HD = 128
SCORE_BOUND = 24.0
EXP2_SCALE = SCORE_BOUND * math.log2(math.e)
GATHER_CHUNKS = 8
QUERY_CHUNKS = 4
AHEAD = 2
MESH = pl.DeviceIdType.MESH


def layer_kernel(
    n, g, tok_hbm, wq_hbm, wv_hbm, wo_hbm, lengths, out_ref,
    tok, w, wo, q, kv, ones, att, from_low, from_high, outgoing, own_sum,
    load_sem, up_send, down_send, tok_recv, kv_send, kv_pass, kv_recv,
    sum_send, low_recv, high_recv,
):
    rows, wide = tok_hbm.shape
    heads = wide // HD
    half = g // 2
    gather_chunks, query_chunks = GATHER_CHUNKS, QUERY_CHUNKS
    step_rows = rows // gather_chunks
    query_rows = rows // query_chunks
    k = lax.axis_index("head")
    ctx = lax.axis_index("ctx")
    doc = ctx // g
    base = doc * g
    j = ctx - base
    partner = j + 1 - 2 * lax.rem(j, 2)

    loads = [
        pltpu.make_async_copy(tok_hbm, tok.at[k], load_sem.at[0]),
        pltpu.make_async_copy(wq_hbm, w.at[:, pl.ds(0, wide)], load_sem.at[1]),
        pltpu.make_async_copy(wv_hbm, w.at[:, pl.ds(wide, wide)], load_sem.at[2]),
        pltpu.make_async_copy(wo_hbm, wo, load_sem.at[3]),
    ]
    for load in loads:
        load.start()

    barrier = pltpu.get_barrier_semaphore()

    def greet(where):
        pl.semaphore_signal(barrier, inc=1, device_id=where, device_id_type=MESH)

    @pl.when(k > 0)
    def _():
        greet({"head": k - 1})

    @pl.when(k < n - 1)
    def _():
        greet({"head": k + 1})

    greet({"ctx": base + partner})
    for m in range(1, half):
        greet({"ctx": base + lax.rem(j + 2 * m, g)})
    pl.semaphore_wait(
        barrier, jnp.where(k > 0, 1, 0) + jnp.where(k < n - 1, 1, 0) + half
    )

    limit = jnp.where(doc == 0, lengths[0], lengths[1])

    def valid_rows(first, count):
        position = first + lax.broadcasted_iota(jnp.int32, (count, HD), 0)
        return jnp.where(position < limit, 1.0, 0.0)

    def chunk(c):
        return pl.ds(pl.multiple_of(c * step_rows, step_rows), step_rows)

    def tok_copy(source, c, to, sends):
        piece = tok.at[source, chunk(c)]
        return pltpu.make_async_remote_copy(
            src_ref=piece, dst_ref=piece, send_sem=sends.at[source, c],
            recv_sem=tok_recv.at[source, c], device_id={"head": to}, device_id_type=MESH,
        )

    def send_tok(source, c, up):
        if up:
            @pl.when(k < n - 1)
            def _():
                tok_copy(source, c, k + 1, up_send).start()
        else:
            @pl.when(k > 0)
            def _():
                tok_copy(source, c, k - 1, down_send).start()

    def arrive(source, c, up):
        tok_copy(source, c, k, up_send).wait_recv()
        send_tok(source, c, up)

    def kv_copy(slot, c, to, sem):
        piece = kv.at[slot, chunk(c)]
        return pltpu.make_async_remote_copy(
            src_ref=piece, dst_ref=piece, send_sem=sem, recv_sem=kv_recv.at[slot, c],
            device_id={"ctx": base + to}, device_id_type=MESH,
        )

    def behind(m):
        return lax.rem(j + g - 2 * m, g)

    def pass_on(c):
        for m in range(1, half):
            slot = behind(m)
            kv_copy(slot, c, partner, kv_pass.at[m, c]).wait_recv()
            kv_copy(slot, c, partner, kv_pass.at[m, c]).start()

    loads[0].wait()
    for c in range(AHEAD):
        send_tok(k, c, True)
        send_tok(k, c, False)
    ones[...] = jnp.concatenate(
        [valid_rows(block * rows, rows) for block in range(g)], axis=0
    ).astype(jnp.bfloat16)
    loads[1].wait()
    loads[2].wait()

    def gather_step(c, carry):
        for distance in range(1, n):
            @pl.when(k - distance >= 0)
            def _():
                arrive(k - distance, c, True)

            @pl.when(k + distance < n)
            def _():
                arrive(k + distance, c, False)

        @pl.when(c + AHEAD < gather_chunks)
        def _():
            send_tok(k, c + AHEAD, True)
            send_tok(k, c + AHEAD, False)

        total = jnp.dot(tok[0, chunk(c)], w[0:wide], preferred_element_type=jnp.float32)
        for s in range(1, n):
            total += jnp.dot(
                tok[s, chunk(c)], w[s * wide:(s + 1) * wide],
                preferred_element_type=jnp.float32,
            )
        valid = valid_rows(j * rows + c * step_rows, step_rows)
        for h in range(heads):
            columns = slice(h * HD, (h + 1) * HD)
            part = total[:, columns]
            unit = part * lax.rsqrt(jnp.sum(part * part, axis=1, keepdims=True) + 1e-06)
            kv[j, chunk(c), columns] = unit.astype(jnp.bfloat16)
            q[chunk(c), columns] = (unit * EXP2_SCALE).astype(jnp.bfloat16)
            shifted = slice(wide + h * HD, wide + (h + 1) * HD)
            kv[j, chunk(c), shifted] = (total[:, shifted] * valid).astype(jnp.bfloat16)
        for m in range(1, half):
            kv_copy(j, c, lax.rem(j + 2 * m, g), kv_send.at[m, c]).start()
        kv_copy(j, c, partner, kv_send.at[0, c]).start()

        @pl.when(c > 0)
        def _():
            pass_on(c - 1)

        return carry

    lax.fori_loop(0, gather_chunks, gather_step, 0)
    pass_on(gather_chunks - 1)
    loads[3].wait()

    def gather_end(c, carry):
        kv_copy(partner, c, partner, kv_send.at[0, c]).wait_recv()
        for m in range(1, half):
            slot = lax.rem(partner + g - 2 * m, g)
            kv_copy(slot, c, partner, kv_pass.at[m, c]).wait_recv()
        return carry

    lax.fori_loop(0, gather_chunks, gather_end, 0)

    def sum_copy(c, d, to, landing, recv):
        return pltpu.make_async_remote_copy(
            src_ref=outgoing.at[c, d], dst_ref=landing.at[c, d], send_sem=sum_send.at[c, d],
            recv_sem=recv.at[c, d], device_id={"head": to}, device_id_type=MESH,
        )

    def query_chunk(c):
        return pl.ds(pl.multiple_of(c * query_rows, query_rows), query_rows)

    def share(d):
        columns = pl.ds(pl.multiple_of(d * wide, HD), wide)
        return jnp.dot(att[...], wo[:, columns], preferred_element_type=jnp.float32)

    def query_step(c, carry):
        own = c * query_rows
        valid = valid_rows(j * rows + own, query_rows)
        row = lax.broadcasted_iota(jnp.int32, (query_rows, rows), 0) + own
        column = lax.broadcasted_iota(jnp.int32, (query_rows, rows), 1)
        for h in range(heads):
            columns = slice(h * HD, (h + 1) * HD)
            shifted = slice(wide + h * HD, wide + (h + 1) * HD)
            queries = q[query_chunk(c), columns]
            total = None
            for b in range(g):
                block = lax.rem(j + b, g)
                scores = lax.dot_general(
                    queries, kv[block, :, columns], (((1,), (1,)), ((), ())),
                    preferred_element_type=jnp.float32,
                )
                weights = jnp.exp2(scores)
                if b == 0:
                    weights = jnp.where(row != column, weights, 0.0)
                block_rows = pl.ds(pl.multiple_of(block * rows, rows), rows)
                values = jnp.concatenate(
                    [kv[block, :, shifted], ones[block_rows]], axis=1
                )
                term = jnp.dot(
                    weights.astype(jnp.bfloat16), values, preferred_element_type=jnp.float32
                )
                total = term if total is None else total + term
            result = valid * total[:, :HD] / (total[:, HD:] + (1.0 - valid))
            att[:, columns] = result.astype(jnp.bfloat16)

        def emit(d, to, waits, landing, recv):
            @pl.when(waits)
            def _():
                sum_copy(c, d, k, landing, recv).wait_recv()
                outgoing[c, d] = (share(d) + landing[c, d].astype(jnp.float32)).astype(
                    jnp.bfloat16
                )

            @pl.when(jnp.logical_not(waits))
            def _():
                outgoing[c, d] = share(d).astype(jnp.bfloat16)

            sum_copy(c, d, to, landing, recv).start()

        for off in range(n - 1, 0, -1):
            @pl.when(k + off < n)
            def _():
                emit(k + off, k + 1, k > 0, from_low, low_recv)

            @pl.when(k - off >= 0)
            def _():
                emit(k - off, k - 1, k < n - 1, from_high, high_recv)

        own_sum[query_chunk(c)] = share(k)
        return carry

    lax.fori_loop(0, query_chunks, query_step, 0)

    def finish(c, carry):
        @pl.when(k > 0)
        def _():
            sum_copy(c, k, k, from_low, low_recv).wait_recv()
            own_sum[query_chunk(c)] += from_low[c, k].astype(jnp.float32)

        @pl.when(k < n - 1)
        def _():
            sum_copy(c, k, k, from_high, high_recv).wait_recv()
            own_sum[query_chunk(c)] += from_high[c, k].astype(jnp.float32)

        out_ref[query_chunk(c)] = own_sum[query_chunk(c)].astype(out_ref.dtype)
        return carry

    lax.fori_loop(0, query_chunks, finish, 0)

    def drain_gather(c, carry):
        for s in range(n):
            @pl.when(jnp.logical_and(s <= k, k < n - 1))
            def _():
                tok_copy(s, c, k + 1, up_send).wait_send()

            @pl.when(jnp.logical_and(s >= k, k > 0))
            def _():
                tok_copy(s, c, k - 1, down_send).wait_send()

        kv_copy(j, c, partner, kv_send.at[0, c]).wait_send()
        for m in range(1, half):
            kv_copy(j, c, partner, kv_send.at[m, c]).wait_send()
            kv_copy(behind(m), c, partner, kv_pass.at[m, c]).wait_send()
        return carry

    lax.fori_loop(0, gather_chunks, drain_gather, 0)

    def drain_sums(c, carry):
        for d in range(n):
            @pl.when(d > k)
            def _():
                sum_copy(c, d, k + 1, from_low, low_recv).wait_send()

            @pl.when(d < k)
            def _():
                sum_copy(c, d, k - 1, from_high, high_recv).wait_send()

        return carry

    lax.fori_loop(0, query_chunks, drain_sums, 0)


def per_device(tokens, w_query, w_value, w_out, doc_lengths):
    n = lax.axis_size("head")
    g = lax.axis_size("ctx") // 2
    rows, wide = tokens.shape
    depth = w_query.shape[0]
    query_rows = rows // QUERY_CHUNKS
    bf16, f32 = jnp.bfloat16, jnp.float32
    dma = pltpu.SemaphoreType.DMA
    any_space = pl.BlockSpec(memory_space=pl.ANY)
    pieces = (QUERY_CHUNKS, n, query_rows, wide)
    return pl.pallas_call(
        functools.partial(layer_kernel, n, g),
        out_shape=jax.ShapeDtypeStruct((rows, wide), bf16),
        in_specs=[any_space] * 4 + [pl.BlockSpec(memory_space=pltpu.SMEM)],
        out_specs=pl.BlockSpec(memory_space=pltpu.VMEM),
        scratch_shapes=[
            pltpu.VMEM((n, rows, wide), bf16),
            pltpu.VMEM((depth, 2 * wide), bf16),
            pltpu.VMEM(w_out.shape, bf16),
            pltpu.VMEM((rows, wide), bf16),
            pltpu.VMEM((g, rows, 2 * wide), bf16),
            pltpu.VMEM((g * rows, HD), bf16),
            pltpu.VMEM((query_rows, wide), bf16),
            pltpu.VMEM(pieces, bf16),
            pltpu.VMEM(pieces, bf16),
            pltpu.VMEM(pieces, bf16),
            pltpu.VMEM((rows, wide), f32),
            dma((4,)),
            dma((n, GATHER_CHUNKS)),
            dma((n, GATHER_CHUNKS)),
            dma((n, GATHER_CHUNKS)),
            dma((g // 2, GATHER_CHUNKS)),
            dma((g // 2, GATHER_CHUNKS)),
            dma((g, GATHER_CHUNKS)),
            dma((QUERY_CHUNKS, n)),
            dma((QUERY_CHUNKS, n)),
            dma((QUERY_CHUNKS, n)),
        ],
        compiler_params=pltpu.CompilerParams(
            collective_id=0, has_side_effects=True, vmem_limit_bytes=60 * 1024 * 1024
        ),
    )(tokens, w_query, w_value, w_out, doc_lengths)


def solution(mesh):
    return jax.shard_map(
        per_device,
        mesh=mesh,
        in_specs=(P("ctx", "head"), P(None, "head"), P(None, "head"), P("head", None), P()),
        out_specs=P("ctx", "head"),
        check_vma=False,
    )
```

```python
import functools
import math

import jax
import jax.numpy as jnp
from jax import lax
from jax.experimental import pallas as pl
from jax.experimental.pallas import tpu as pltpu
from jax.sharding import PartitionSpec as P

HD = 128
SCORE_BOUND = 24.0
EXP2_SCALE = SCORE_BOUND * math.log2(math.e)
GATHER_CHUNKS = 8
QUERY_CHUNKS = 4
AHEAD = 2
MESH = pl.DeviceIdType.MESH


def layer_kernel(
    n, g, tok_hbm, wq_hbm, wv_hbm, wo_hbm, lengths, out_ref,
    tok, w, wo, q, kv, ones, att, from_low, from_high, outgoing, own_sum, spread, wo_own,
    load_sem, up_send, down_send, tok_recv, kv_send, kv_pass, kv_recv,
    sum_send, low_recv, high_recv, spread_up, spread_down, spread_recv,
    deal_send, share_send, wo_recv,
):
    rows, wide = tok_hbm.shape
    heads = wide // HD
    half = g // 2
    ctx_count = 2 * g
    deal_rows = wide // ctx_count
    gather_chunks, query_chunks = GATHER_CHUNKS, QUERY_CHUNKS
    step_rows = rows // gather_chunks
    query_rows = rows // query_chunks
    k = lax.axis_index("head")
    ctx = lax.axis_index("ctx")
    doc = ctx // g
    base = doc * g
    j = ctx - base
    partner = j + 1 - 2 * lax.rem(j, 2)

    loads = [
        pltpu.make_async_copy(tok_hbm, tok.at[k], load_sem.at[0]),
        pltpu.make_async_copy(wq_hbm, w.at[:, pl.ds(0, wide)], load_sem.at[1]),
        pltpu.make_async_copy(wv_hbm, w.at[:, pl.ds(wide, wide)], load_sem.at[2]),
        pltpu.make_async_copy(wo_hbm, wo, load_sem.at[3]),
        pltpu.make_async_copy(
            wo_hbm.at[:, pl.ds(pl.multiple_of(k * wide, HD), wide)], wo_own.at[k], load_sem.at[4]
        ),
    ]
    for load in loads:
        load.start()

    barrier = pltpu.get_barrier_semaphore()

    def greet(where):
        pl.semaphore_signal(barrier, inc=1, device_id=where, device_id_type=MESH)

    for m in range(1, n):
        greet({"head": lax.rem(k + m, n)})
    for m in range(1, ctx_count):
        greet({"ctx": lax.rem(ctx + m, ctx_count)})
    pl.semaphore_wait(barrier, n + ctx_count - 2)

    limit = jnp.where(doc == 0, lengths[0], lengths[1])

    def valid_rows(first, count):
        position = first + lax.broadcasted_iota(jnp.int32, (count, HD), 0)
        return jnp.where(position < limit, 1.0, 0.0)

    def chunk(c):
        return pl.ds(pl.multiple_of(c * step_rows, step_rows), step_rows)

    def tok_copy(source, c, to, sends):
        piece = tok.at[source, chunk(c)]
        return pltpu.make_async_remote_copy(
            src_ref=piece, dst_ref=piece, send_sem=sends.at[source, c],
            recv_sem=tok_recv.at[source, c], device_id={"head": to}, device_id_type=MESH,
        )

    def send_tok(source, c, up):
        if up:
            @pl.when(k < n - 1)
            def _():
                tok_copy(source, c, k + 1, up_send).start()
        else:
            @pl.when(k > 0)
            def _():
                tok_copy(source, c, k - 1, down_send).start()

    def arrive(source, c, up):
        tok_copy(source, c, k, up_send).wait_recv()
        send_tok(source, c, up)

    def kv_copy(slot, c, to, sem):
        piece = kv.at[slot, chunk(c)]
        return pltpu.make_async_remote_copy(
            src_ref=piece, dst_ref=piece, send_sem=sem, recv_sem=kv_recv.at[slot, c],
            device_id={"ctx": base + to}, device_id_type=MESH,
        )

    def behind(m):
        return lax.rem(j + g - 2 * m, g)

    def pass_on(c):
        for m in range(1, half):
            slot = behind(m)
            kv_copy(slot, c, partner, kv_pass.at[m, c]).wait_recv()
            kv_copy(slot, c, partner, kv_pass.at[m, c]).start()

    loads[0].wait()
    for c in range(AHEAD):
        send_tok(k, c, True)
        send_tok(k, c, False)
    ones[...] = jnp.concatenate(
        [valid_rows(block * rows, rows) for block in range(g)], axis=0
    ).astype(jnp.bfloat16)
    loads[1].wait()
    loads[2].wait()

    def gather_step(c, carry):
        for distance in range(1, n):
            @pl.when(k - distance >= 0)
            def _():
                arrive(k - distance, c, True)

            @pl.when(k + distance < n)
            def _():
                arrive(k + distance, c, False)

        @pl.when(c + AHEAD < gather_chunks)
        def _():
            send_tok(k, c + AHEAD, True)
            send_tok(k, c + AHEAD, False)

        total = jnp.dot(tok[0, chunk(c)], w[0:wide], preferred_element_type=jnp.float32)
        for s in range(1, n):
            total += jnp.dot(
                tok[s, chunk(c)], w[s * wide:(s + 1) * wide],
                preferred_element_type=jnp.float32,
            )
        valid = valid_rows(j * rows + c * step_rows, step_rows)
        for h in range(heads):
            columns = slice(h * HD, (h + 1) * HD)
            part = total[:, columns]
            unit = part * lax.rsqrt(jnp.sum(part * part, axis=1, keepdims=True) + 1e-06)
            kv[j, chunk(c), columns] = unit.astype(jnp.bfloat16)
            q[chunk(c), columns] = (unit * EXP2_SCALE).astype(jnp.bfloat16)
            shifted = slice(wide + h * HD, wide + (h + 1) * HD)
            kv[j, chunk(c), shifted] = (total[:, shifted] * valid).astype(jnp.bfloat16)
        for m in range(1, half):
            kv_copy(j, c, lax.rem(j + 2 * m, g), kv_send.at[m, c]).start()
        kv_copy(j, c, partner, kv_send.at[0, c]).start()

        @pl.when(c > 0)
        def _():
            pass_on(c - 1)

        return carry

    lax.fori_loop(0, gather_chunks, gather_step, 0)
    pass_on(gather_chunks - 1)
    loads[3].wait()
    loads[4].wait()

    def deal_copy(d):
        mine = pl.ds(pl.multiple_of(ctx * deal_rows, deal_rows), deal_rows)
        return pltpu.make_async_remote_copy(
            src_ref=wo.at[mine, pl.ds(pl.multiple_of(d * wide, HD), wide)],
            dst_ref=wo_own.at[k, mine], send_sem=deal_send.at[d], recv_sem=wo_recv.at[k, ctx],
            device_id={"head": d}, device_id_type=MESH,
        )

    def share_copy(source, dealer, to):
        piece = wo_own.at[
            source, pl.ds(pl.multiple_of(dealer * deal_rows, deal_rows), deal_rows)
        ]
        return pltpu.make_async_remote_copy(
            src_ref=piece, dst_ref=piece, send_sem=share_send.at[source, to],
            recv_sem=wo_recv.at[source, dealer], device_id={"ctx": to}, device_id_type=MESH,
        )

    def other(m):
        return lax.rem(ctx + m, ctx_count)

    for m in range(1, n):
        deal_copy(lax.rem(k + m, n)).start()

    def gather_end(c, carry):
        kv_copy(partner, c, partner, kv_send.at[0, c]).wait_recv()
        for m in range(1, half):
            slot = lax.rem(partner + g - 2 * m, g)
            kv_copy(slot, c, partner, kv_pass.at[m, c]).wait_recv()
        return carry

    lax.fori_loop(0, gather_chunks, gather_end, 0)

    def sum_copy(c, d, to, landing, recv):
        return pltpu.make_async_remote_copy(
            src_ref=outgoing.at[c, d], dst_ref=landing.at[c, d], send_sem=sum_send.at[c, d],
            recv_sem=recv.at[c, d], device_id={"head": to}, device_id_type=MESH,
        )

    def query_chunk(c):
        return pl.ds(pl.multiple_of(c * query_rows, query_rows), query_rows)

    def share(d):
        columns = pl.ds(pl.multiple_of(d * wide, HD), wide)
        return jnp.dot(att[...], wo[:, columns], preferred_element_type=jnp.float32)

    def attend(c, target):
        own = c * query_rows
        valid = valid_rows(j * rows + own, query_rows)
        row = lax.broadcasted_iota(jnp.int32, (query_rows, rows), 0) + own
        column = lax.broadcasted_iota(jnp.int32, (query_rows, rows), 1)
        for h in range(heads):
            columns = slice(h * HD, (h + 1) * HD)
            shifted = slice(wide + h * HD, wide + (h + 1) * HD)
            queries = q[query_chunk(c), columns]
            total = None
            for b in range(g):
                block = lax.rem(j + b, g)
                scores = lax.dot_general(
                    queries, kv[block, :, columns], (((1,), (1,)), ((), ())),
                    preferred_element_type=jnp.float32,
                )
                weights = jnp.exp2(scores)
                if b == 0:
                    weights = jnp.where(row != column, weights, 0.0)
                block_rows = pl.ds(pl.multiple_of(block * rows, rows), rows)
                values = jnp.concatenate(
                    [kv[block, :, shifted], ones[block_rows]], axis=1
                )
                term = jnp.dot(
                    weights.astype(jnp.bfloat16), values, preferred_element_type=jnp.float32
                )
                total = term if total is None else total + term
            result = valid * total[:, :HD] / (total[:, HD:] + (1.0 - valid))
            target[:, columns] = result.astype(jnp.bfloat16)

    def emit(c, d, to, waits, landing, recv):
        @pl.when(waits)
        def _():
            sum_copy(c, d, k, landing, recv).wait_recv()
            outgoing[c, d] = (share(d) + landing[c, d].astype(jnp.float32)).astype(jnp.bfloat16)

        @pl.when(jnp.logical_not(waits))
        def _():
            outgoing[c, d] = share(d).astype(jnp.bfloat16)

        sum_copy(c, d, to, landing, recv).start()

    def spread_copy(c, s, to, sends):
        piece = spread.at[c, s]
        return pltpu.make_async_remote_copy(
            src_ref=piece, dst_ref=piece, send_sem=sends.at[c, s],
            recv_sem=spread_recv.at[c, s], device_id={"head": to}, device_id_type=MESH,
        )

    def relay(c, distance):
        @pl.when(jnp.logical_and(k - distance >= 0, k < n - 1))
        def _():
            spread_copy(c, k - distance, k, spread_up).wait_recv()
            spread_copy(c, k - distance, k + 1, spread_up).start()

        @pl.when(jnp.logical_and(k + distance < n, k > 0))
        def _():
            spread_copy(c, k + distance, k, spread_down).wait_recv()
            spread_copy(c, k + distance, k - 1, spread_down).start()

    def pair_step(c, carry):
        attend(2 * c, spread.at[c, k])

        @pl.when(k < n - 1)
        def _():
            spread_copy(c, k, k + 1, spread_up).start()

        @pl.when(k > 0)
        def _():
            spread_copy(c, k, k - 1, spread_down).start()

        @pl.when(c == 0)
        def _():
            for m in range(1, n):
                source = lax.rem(k + m, n)
                share_copy(source, ctx, ctx).wait_recv()

                def hand_out(step, inner):
                    share_copy(source, ctx, other(step)).start()
                    return inner

                lax.fori_loop(1, ctx_count, hand_out, 0)

        attend(2 * c + 1, att)
        relay(c, 1)
        for off in range(n - 1, 0, -1):
            @pl.when(k + off < n)
            def _():
                emit(c, k + off, k + 1, k > 0, from_low, low_recv)

            @pl.when(k - off >= 0)
            def _():
                emit(c, k - off, k - 1, k < n - 1, from_high, high_recv)

        own_sum[c] = share(k)
        for distance in range(2, n):
            relay(c, distance)
        return carry

    pairs = query_chunks // 2
    lax.fori_loop(0, pairs, pair_step, 0)

    def collect(step, carry):
        for m in range(1, n):
            share_copy(lax.rem(k + m, n), other(step), ctx).wait_recv()
        return carry

    lax.fori_loop(1, ctx_count, collect, 0)

    def finish(c, carry):
        for distance in range(1, n):
            @pl.when(jnp.logical_and(k - distance >= 0, k == n - 1))
            def _():
                spread_copy(c, k - distance, k, spread_up).wait_recv()

            @pl.when(jnp.logical_and(k + distance < n, k == 0))
            def _():
                spread_copy(c, k + distance, k, spread_down).wait_recv()

        total = jnp.dot(spread[c, 0], wo_own[0], preferred_element_type=jnp.float32)
        for s in range(1, n):
            total += jnp.dot(spread[c, s], wo_own[s], preferred_element_type=jnp.float32)
        out_ref[query_chunk(2 * c)] = total.astype(out_ref.dtype)

        @pl.when(k > 0)
        def _():
            sum_copy(c, k, k, from_low, low_recv).wait_recv()
            own_sum[c] += from_low[c, k].astype(jnp.float32)

        @pl.when(k < n - 1)
        def _():
            sum_copy(c, k, k, from_high, high_recv).wait_recv()
            own_sum[c] += from_high[c, k].astype(jnp.float32)

        out_ref[query_chunk(2 * c + 1)] = own_sum[c].astype(out_ref.dtype)
        return carry

    lax.fori_loop(0, pairs, finish, 0)

    def drain_gather(c, carry):
        for s in range(n):
            @pl.when(jnp.logical_and(s <= k, k < n - 1))
            def _():
                tok_copy(s, c, k + 1, up_send).wait_send()

            @pl.when(jnp.logical_and(s >= k, k > 0))
            def _():
                tok_copy(s, c, k - 1, down_send).wait_send()

        kv_copy(j, c, partner, kv_send.at[0, c]).wait_send()
        for m in range(1, half):
            kv_copy(j, c, partner, kv_send.at[m, c]).wait_send()
            kv_copy(behind(m), c, partner, kv_pass.at[m, c]).wait_send()
        return carry

    lax.fori_loop(0, gather_chunks, drain_gather, 0)

    def drain_sums(c, carry):
        for d in range(n):
            @pl.when(d > k)
            def _():
                sum_copy(c, d, k + 1, from_low, low_recv).wait_send()

            @pl.when(d < k)
            def _():
                sum_copy(c, d, k - 1, from_high, high_recv).wait_send()

            @pl.when(jnp.logical_and(d <= k, k < n - 1))
            def _():
                spread_copy(c, d, k + 1, spread_up).wait_send()

            @pl.when(jnp.logical_and(d >= k, k > 0))
            def _():
                spread_copy(c, d, k - 1, spread_down).wait_send()

        return carry

    lax.fori_loop(0, pairs, drain_sums, 0)
    for m in range(1, n):
        deal_copy(lax.rem(k + m, n)).wait_send()

    def drain_shares(step, carry):
        for m in range(1, n):
            share_copy(lax.rem(k + m, n), ctx, other(step)).wait_send()
        return carry

    lax.fori_loop(1, ctx_count, drain_shares, 0)


def per_device(tokens, w_query, w_value, w_out, doc_lengths):
    n = lax.axis_size("head")
    g = lax.axis_size("ctx") // 2
    rows, wide = tokens.shape
    depth = w_query.shape[0]
    query_rows = rows // QUERY_CHUNKS
    bf16, f32 = jnp.bfloat16, jnp.float32
    dma = pltpu.SemaphoreType.DMA
    any_space = pl.BlockSpec(memory_space=pl.ANY)
    pairs = QUERY_CHUNKS // 2
    pieces = (pairs, n, query_rows, wide)
    return pl.pallas_call(
        functools.partial(layer_kernel, n, g),
        out_shape=jax.ShapeDtypeStruct((rows, wide), bf16),
        in_specs=[any_space] * 4 + [pl.BlockSpec(memory_space=pltpu.SMEM)],
        out_specs=pl.BlockSpec(memory_space=pltpu.VMEM),
        scratch_shapes=[
            pltpu.VMEM((n, rows, wide), bf16),
            pltpu.VMEM((depth, 2 * wide), bf16),
            pltpu.VMEM(w_out.shape, bf16),
            pltpu.VMEM((rows, wide), bf16),
            pltpu.VMEM((g, rows, 2 * wide), bf16),
            pltpu.VMEM((g * rows, HD), bf16),
            pltpu.VMEM((query_rows, wide), bf16),
            pltpu.VMEM(pieces, bf16),
            pltpu.VMEM(pieces, bf16),
            pltpu.VMEM(pieces, bf16),
            pltpu.VMEM((pairs, query_rows, wide), f32),
            pltpu.VMEM(pieces, bf16),
            pltpu.VMEM((n, wide, wide), bf16),
            dma((5,)),
            dma((n, GATHER_CHUNKS)),
            dma((n, GATHER_CHUNKS)),
            dma((n, GATHER_CHUNKS)),
            dma((g // 2, GATHER_CHUNKS)),
            dma((g // 2, GATHER_CHUNKS)),
            dma((g, GATHER_CHUNKS)),
            dma((pairs, n)),
            dma((pairs, n)),
            dma((pairs, n)),
            dma((pairs, n)),
            dma((pairs, n)),
            dma((pairs, n)),
            dma((n,)),
            dma((n, 2 * g)),
            dma((n, 2 * g)),
        ],
        compiler_params=pltpu.CompilerParams(
            collective_id=0, has_side_effects=True, vmem_limit_bytes=60 * 1024 * 1024
        ),
    )(tokens, w_query, w_value, w_out, doc_lengths)


def solution(mesh):
    return jax.shard_map(
        per_device,
        mesh=mesh,
        in_specs=(P("ctx", "head"), P(None, "head"), P(None, "head"), P("head", None), P()),
        out_specs=P("ctx", "head"),
        check_vma=False,
    )
```

```python
import functools
import math

import jax
import jax.numpy as jnp
from jax import lax
from jax.experimental import pallas as pl
from jax.experimental.pallas import tpu as pltpu
from jax.sharding import PartitionSpec as P

HD = 128
SCORE_BOUND = 24.0
EXP2_SCALE = SCORE_BOUND * math.log2(math.e)
GATHER_CHUNKS = 8
QUERY_CHUNKS = 4
AHEAD = 2
MESH = pl.DeviceIdType.MESH


def layer_kernel(
    n, g, tok_hbm, wq_hbm, wv_hbm, wo_hbm, lengths, out_ref,
    tok, w, wo, q, kv, ones, att, from_low, from_high, outgoing, own_sum, spread, wo_own, projected, mixed,
    load_sem, up_send, down_send, tok_recv, kv_send, kv_pass, kv_recv,
    sum_send, low_recv, high_recv, spread_up, spread_down, spread_recv,
    deal_send, share_send, wo_recv,
):
    rows, wide = tok_hbm.shape
    heads = wide // HD
    half = g // 2
    ctx_count = 2 * g
    deal_rows = wide // ctx_count
    gather_chunks, query_chunks = GATHER_CHUNKS, QUERY_CHUNKS
    step_rows = rows // gather_chunks
    query_rows = rows // query_chunks
    k = lax.axis_index("head")
    ctx = lax.axis_index("ctx")
    doc = ctx // g
    base = doc * g
    j = ctx - base
    partner = j + 1 - 2 * lax.rem(j, 2)

    loads = [
        pltpu.make_async_copy(tok_hbm, tok.at[k], load_sem.at[0]),
        pltpu.make_async_copy(wq_hbm, w.at[:, pl.ds(0, wide)], load_sem.at[1]),
        pltpu.make_async_copy(wv_hbm, w.at[:, pl.ds(wide, wide)], load_sem.at[2]),
        pltpu.make_async_copy(wo_hbm, wo, load_sem.at[3]),
        pltpu.make_async_copy(
            wo_hbm.at[:, pl.ds(pl.multiple_of(k * wide, HD), wide)], wo_own.at[k], load_sem.at[4]
        ),
    ]
    for load in loads:
        load.start()

    barrier = pltpu.get_barrier_semaphore()

    def greet(where):
        pl.semaphore_signal(barrier, inc=1, device_id=where, device_id_type=MESH)

    for m in range(1, n):
        greet({"head": lax.rem(k + m, n)})
    for m in range(1, ctx_count):
        greet({"ctx": lax.rem(ctx + m, ctx_count)})
    pl.semaphore_wait(barrier, n + ctx_count - 2)

    limit = jnp.where(doc == 0, lengths[0], lengths[1])

    def valid_rows(first, count):
        position = first + lax.broadcasted_iota(jnp.int32, (count, HD), 0)
        return jnp.where(position < limit, 1.0, 0.0)

    def chunk(c):
        return pl.ds(pl.multiple_of(c * step_rows, step_rows), step_rows)

    def tok_copy(source, c, to, sends):
        piece = tok.at[source, chunk(c)]
        return pltpu.make_async_remote_copy(
            src_ref=piece, dst_ref=piece, send_sem=sends.at[source, c],
            recv_sem=tok_recv.at[source, c], device_id={"head": to}, device_id_type=MESH,
        )

    def send_tok(source, c, up):
        if up:
            @pl.when(k < n - 1)
            def _():
                tok_copy(source, c, k + 1, up_send).start()
        else:
            @pl.when(k > 0)
            def _():
                tok_copy(source, c, k - 1, down_send).start()

    def arrive(source, c, up):
        tok_copy(source, c, k, up_send).wait_recv()
        send_tok(source, c, up)

    def kv_copy(slot, c, to, sem):
        piece = kv.at[slot, chunk(c)]
        return pltpu.make_async_remote_copy(
            src_ref=piece, dst_ref=piece, send_sem=sem, recv_sem=kv_recv.at[slot, c],
            device_id={"ctx": base + to}, device_id_type=MESH,
        )

    def behind(m):
        return lax.rem(j + g - 2 * m, g)

    def pass_on(c):
        for m in range(1, half):
            slot = behind(m)
            kv_copy(slot, c, partner, kv_pass.at[m, c]).wait_recv()
            kv_copy(slot, c, partner, kv_pass.at[m, c]).start()

    loads[0].wait()
    for c in range(AHEAD):
        send_tok(k, c, True)
        send_tok(k, c, False)
    ones[...] = jnp.concatenate(
        [valid_rows(block * rows, rows) for block in range(g)], axis=0
    ).astype(jnp.bfloat16)
    loads[1].wait()
    loads[2].wait()

    def gather_step(c, carry):
        def product(source):
            depth = pl.ds(pl.multiple_of(source * wide, HD), wide)
            return jnp.dot(tok[source, chunk(c)], w[depth], preferred_element_type=jnp.float32)

        projected[...] = product(k)
        for distance in range(1, n):
            @pl.when(k - distance >= 0)
            def _():
                arrive(k - distance, c, True)

            @pl.when(k + distance < n)
            def _():
                arrive(k + distance, c, False)

            @pl.when(k - distance >= 0)
            def _():
                projected[...] += product(k - distance)

            @pl.when(k + distance < n)
            def _():
                projected[...] += product(k + distance)

        @pl.when(c + AHEAD < gather_chunks)
        def _():
            send_tok(k, c + AHEAD, True)
            send_tok(k, c + AHEAD, False)

        total = projected[...]
        valid = valid_rows(j * rows + c * step_rows, step_rows)
        for h in range(heads):
            columns = slice(h * HD, (h + 1) * HD)
            part = total[:, columns]
            unit = part * lax.rsqrt(jnp.sum(part * part, axis=1, keepdims=True) + 1e-06)
            kv[j, chunk(c), columns] = unit.astype(jnp.bfloat16)
            q[chunk(c), columns] = (unit * EXP2_SCALE).astype(jnp.bfloat16)
            shifted = slice(wide + h * HD, wide + (h + 1) * HD)
            kv[j, chunk(c), shifted] = (total[:, shifted] * valid).astype(jnp.bfloat16)
        for m in range(1, half):
            kv_copy(j, c, lax.rem(j + 2 * m, g), kv_send.at[m, c]).start()
        kv_copy(j, c, partner, kv_send.at[0, c]).start()

        @pl.when(c > 0)
        def _():
            pass_on(c - 1)

        return carry

    lax.fori_loop(0, gather_chunks, gather_step, 0)
    loads[3].wait()
    loads[4].wait()

    def deal_copy(d):
        mine = pl.ds(pl.multiple_of(ctx * deal_rows, deal_rows), deal_rows)
        return pltpu.make_async_remote_copy(
            src_ref=wo.at[mine, pl.ds(pl.multiple_of(d * wide, HD), wide)],
            dst_ref=wo_own.at[k, mine], send_sem=deal_send.at[d], recv_sem=wo_recv.at[k, ctx],
            device_id={"head": d}, device_id_type=MESH,
        )

    def share_copy(source, dealer, to):
        piece = wo_own.at[
            source, pl.ds(pl.multiple_of(dealer * deal_rows, deal_rows), deal_rows)
        ]
        return pltpu.make_async_remote_copy(
            src_ref=piece, dst_ref=piece, send_sem=share_send.at[source, to],
            recv_sem=wo_recv.at[source, dealer], device_id={"ctx": to}, device_id_type=MESH,
        )

    def other(m):
        return lax.rem(ctx + m, ctx_count)

    for m in range(1, n):
        deal_copy(lax.rem(k + m, n)).start()

    def settle(slot):
        def landed(c, carry):
            kv_copy(slot, c, partner, kv_send.at[0, c]).wait_recv()
            return carry

        lax.fori_loop(0, gather_chunks, landed, 0)

    blocks = [j, partner]
    blocks += [behind(m) for m in range(1, half)]
    blocks += [lax.rem(partner + g - 2 * m, g) for m in range(1, half)]

    def sum_copy(c, d, to, landing, recv):
        return pltpu.make_async_remote_copy(
            src_ref=outgoing.at[c, d], dst_ref=landing.at[c, d], send_sem=sum_send.at[c, d],
            recv_sem=recv.at[c, d], device_id={"head": to}, device_id_type=MESH,
        )

    def query_chunk(c):
        return pl.ds(pl.multiple_of(c * query_rows, query_rows), query_rows)

    def share(d):
        columns = pl.ds(pl.multiple_of(d * wide, HD), wide)
        return jnp.dot(att[...], wo[:, columns], preferred_element_type=jnp.float32)

    def attend(c, target):
        own = c * query_rows
        valid = valid_rows(j * rows + own, query_rows)
        row = lax.broadcasted_iota(jnp.int32, (query_rows, rows), 0) + own
        column = lax.broadcasted_iota(jnp.int32, (query_rows, rows), 1)
        for b, block in enumerate(blocks):
            if b == 1 or b > half:
                @pl.when(c == 0)
                def _():
                    settle(block)
            if b == 2:
                @pl.when(c == 0)
                def _():
                    pass_on(gather_chunks - 1)

            block_rows = pl.ds(pl.multiple_of(block * rows, rows), rows)
            for h in range(heads):
                columns = slice(h * HD, (h + 1) * HD)
                shifted = slice(wide + h * HD, wide + (h + 1) * HD)
                scores = lax.dot_general(
                    q[query_chunk(c), columns], kv[block, :, columns],
                    (((1,), (1,)), ((), ())), preferred_element_type=jnp.float32,
                )
                weights = jnp.exp2(scores)
                if b == 0:
                    weights = jnp.where(row != column, weights, 0.0)
                values = jnp.concatenate(
                    [kv[block, :, shifted], ones[block_rows]], axis=1
                )
                term = jnp.dot(
                    weights.astype(jnp.bfloat16), values, preferred_element_type=jnp.float32
                )
                if b == 0:
                    mixed[h] = term
                else:
                    mixed[h] += term
        for h in range(heads):
            result = valid * mixed[h, :, :HD] / (mixed[h, :, HD:] + (1.0 - valid))
            target[:, h * HD:(h + 1) * HD] = result.astype(jnp.bfloat16)

    def emit(c, d, to, waits, landing, recv):
        @pl.when(waits)
        def _():
            sum_copy(c, d, k, landing, recv).wait_recv()
            outgoing[c, d] = (share(d) + landing[c, d].astype(jnp.float32)).astype(jnp.bfloat16)

        @pl.when(jnp.logical_not(waits))
        def _():
            outgoing[c, d] = share(d).astype(jnp.bfloat16)

        sum_copy(c, d, to, landing, recv).start()

    def spread_copy(c, s, to, sends):
        piece = spread.at[c, s]
        return pltpu.make_async_remote_copy(
            src_ref=piece, dst_ref=piece, send_sem=sends.at[c, s],
            recv_sem=spread_recv.at[c, s], device_id={"head": to}, device_id_type=MESH,
        )

    def relay(c, distance):
        @pl.when(jnp.logical_and(k - distance >= 0, k < n - 1))
        def _():
            spread_copy(c, k - distance, k, spread_up).wait_recv()
            spread_copy(c, k - distance, k + 1, spread_up).start()

        @pl.when(jnp.logical_and(k + distance < n, k > 0))
        def _():
            spread_copy(c, k + distance, k, spread_down).wait_recv()
            spread_copy(c, k + distance, k - 1, spread_down).start()

    def pair_step(c, carry):
        attend(2 * c, spread.at[c, k])

        @pl.when(k < n - 1)
        def _():
            spread_copy(c, k, k + 1, spread_up).start()

        @pl.when(k > 0)
        def _():
            spread_copy(c, k, k - 1, spread_down).start()

        @pl.when(c == 0)
        def _():
            for m in range(1, n):
                source = lax.rem(k + m, n)
                share_copy(source, ctx, ctx).wait_recv()

                def hand_out(step, inner):
                    share_copy(source, ctx, other(step)).start()
                    return inner

                lax.fori_loop(1, ctx_count, hand_out, 0)

        attend(2 * c + 1, att)
        relay(c, 1)
        for off in range(n - 1, 0, -1):
            @pl.when(k + off < n)
            def _():
                emit(c, k + off, k + 1, k > 0, from_low, low_recv)

            @pl.when(k - off >= 0)
            def _():
                emit(c, k - off, k - 1, k < n - 1, from_high, high_recv)

        own_sum[c] = share(k)
        for distance in range(2, n):
            relay(c, distance)
        return carry

    pairs = query_chunks // 2
    lax.fori_loop(0, pairs, pair_step, 0)

    def collect(step, carry):
        for m in range(1, n):
            share_copy(lax.rem(k + m, n), other(step), ctx).wait_recv()
        return carry

    lax.fori_loop(1, ctx_count, collect, 0)

    def finish(c, carry):
        for distance in range(1, n):
            @pl.when(jnp.logical_and(k - distance >= 0, k == n - 1))
            def _():
                spread_copy(c, k - distance, k, spread_up).wait_recv()

            @pl.when(jnp.logical_and(k + distance < n, k == 0))
            def _():
                spread_copy(c, k + distance, k, spread_down).wait_recv()

        total = jnp.dot(spread[c, 0], wo_own[0], preferred_element_type=jnp.float32)
        for s in range(1, n):
            total += jnp.dot(spread[c, s], wo_own[s], preferred_element_type=jnp.float32)
        out_ref[query_chunk(2 * c)] = total.astype(out_ref.dtype)

        @pl.when(k > 0)
        def _():
            sum_copy(c, k, k, from_low, low_recv).wait_recv()
            own_sum[c] += from_low[c, k].astype(jnp.float32)

        @pl.when(k < n - 1)
        def _():
            sum_copy(c, k, k, from_high, high_recv).wait_recv()
            own_sum[c] += from_high[c, k].astype(jnp.float32)

        out_ref[query_chunk(2 * c + 1)] = own_sum[c].astype(out_ref.dtype)
        return carry

    lax.fori_loop(0, pairs, finish, 0)

    def drain_gather(c, carry):
        for s in range(n):
            @pl.when(jnp.logical_and(s <= k, k < n - 1))
            def _():
                tok_copy(s, c, k + 1, up_send).wait_send()

            @pl.when(jnp.logical_and(s >= k, k > 0))
            def _():
                tok_copy(s, c, k - 1, down_send).wait_send()

        kv_copy(j, c, partner, kv_send.at[0, c]).wait_send()
        for m in range(1, half):
            kv_copy(j, c, partner, kv_send.at[m, c]).wait_send()
            kv_copy(behind(m), c, partner, kv_pass.at[m, c]).wait_send()
        return carry

    lax.fori_loop(0, gather_chunks, drain_gather, 0)

    def drain_sums(c, carry):
        for d in range(n):
            @pl.when(d > k)
            def _():
                sum_copy(c, d, k + 1, from_low, low_recv).wait_send()

            @pl.when(d < k)
            def _():
                sum_copy(c, d, k - 1, from_high, high_recv).wait_send()

            @pl.when(jnp.logical_and(d <= k, k < n - 1))
            def _():
                spread_copy(c, d, k + 1, spread_up).wait_send()

            @pl.when(jnp.logical_and(d >= k, k > 0))
            def _():
                spread_copy(c, d, k - 1, spread_down).wait_send()

        return carry

    lax.fori_loop(0, pairs, drain_sums, 0)
    for m in range(1, n):
        deal_copy(lax.rem(k + m, n)).wait_send()

    def drain_shares(step, carry):
        for m in range(1, n):
            share_copy(lax.rem(k + m, n), ctx, other(step)).wait_send()
        return carry

    lax.fori_loop(1, ctx_count, drain_shares, 0)


def per_device(tokens, w_query, w_value, w_out, doc_lengths):
    n = lax.axis_size("head")
    g = lax.axis_size("ctx") // 2
    rows, wide = tokens.shape
    depth = w_query.shape[0]
    query_rows = rows // QUERY_CHUNKS
    bf16, f32 = jnp.bfloat16, jnp.float32
    dma = pltpu.SemaphoreType.DMA
    any_space = pl.BlockSpec(memory_space=pl.ANY)
    pairs = QUERY_CHUNKS // 2
    pieces = (pairs, n, query_rows, wide)
    return pl.pallas_call(
        functools.partial(layer_kernel, n, g),
        out_shape=jax.ShapeDtypeStruct((rows, wide), bf16),
        in_specs=[any_space] * 4 + [pl.BlockSpec(memory_space=pltpu.SMEM)],
        out_specs=pl.BlockSpec(memory_space=pltpu.VMEM),
        scratch_shapes=[
            pltpu.VMEM((n, rows, wide), bf16),
            pltpu.VMEM((depth, 2 * wide), bf16),
            pltpu.VMEM(w_out.shape, bf16),
            pltpu.VMEM((rows, wide), bf16),
            pltpu.VMEM((g, rows, 2 * wide), bf16),
            pltpu.VMEM((g * rows, HD), bf16),
            pltpu.VMEM((query_rows, wide), bf16),
            pltpu.VMEM(pieces, bf16),
            pltpu.VMEM(pieces, bf16),
            pltpu.VMEM(pieces, bf16),
            pltpu.VMEM((pairs, query_rows, wide), f32),
            pltpu.VMEM(pieces, bf16),
            pltpu.VMEM((n, wide, wide), bf16),
            pltpu.VMEM((rows // GATHER_CHUNKS, 2 * wide), f32),
            pltpu.VMEM((wide // HD, query_rows, 2 * HD), f32),
            dma((5,)),
            dma((n, GATHER_CHUNKS)),
            dma((n, GATHER_CHUNKS)),
            dma((n, GATHER_CHUNKS)),
            dma((g // 2, GATHER_CHUNKS)),
            dma((g // 2, GATHER_CHUNKS)),
            dma((g, GATHER_CHUNKS)),
            dma((pairs, n)),
            dma((pairs, n)),
            dma((pairs, n)),
            dma((pairs, n)),
            dma((pairs, n)),
            dma((pairs, n)),
            dma((n,)),
            dma((n, 2 * g)),
            dma((n, 2 * g)),
        ],
        compiler_params=pltpu.CompilerParams(
            collective_id=0, has_side_effects=True, vmem_limit_bytes=60 * 1024 * 1024
        ),
    )(tokens, w_query, w_value, w_out, doc_lengths)


def solution(mesh):
    return jax.shard_map(
        per_device,
        mesh=mesh,
        in_specs=(P("ctx", "head"), P(None, "head"), P(None, "head"), P("head", None), P()),
        out_specs=P("ctx", "head"),
        check_vma=False,
    )
```

```python
import functools
import math

import jax
import jax.numpy as jnp
from jax import lax
from jax.experimental import pallas as pl
from jax.experimental.pallas import tpu as pltpu
from jax.sharding import PartitionSpec as P

HD = 128
SCORE_BOUND = 24.0
EXP2_SCALE = SCORE_BOUND * math.log2(math.e)
GATHER_CHUNKS = 8
QUERY_CHUNKS = 8
AHEAD = 2
MESH = pl.DeviceIdType.MESH


def layer_kernel(
    n, g, tok_hbm, wq_hbm, wv_hbm, wo_hbm, lengths, out_ref,
    tok, w, wo, q, kv, ones, att, from_low, from_high, outgoing, own_sum, spread, wo_own, projected, mixed,
    load_sem, up_send, down_send, tok_recv, kv_send, kv_pass, kv_recv,
    sum_send, low_recv, high_recv, spread_up, spread_down, spread_recv,
    deal_send, share_send, wo_recv,
):
    rows, wide = tok_hbm.shape
    heads = wide // HD
    half = g // 2
    ctx_count = 2 * g
    deal_rows = wide // ctx_count
    gather_chunks, query_chunks = GATHER_CHUNKS, QUERY_CHUNKS
    step_rows = rows // gather_chunks
    query_rows = rows // query_chunks
    k = lax.axis_index("head")
    ctx = lax.axis_index("ctx")
    doc = ctx // g
    base = doc * g
    j = ctx - base
    partner = j + 1 - 2 * lax.rem(j, 2)

    loads = [
        pltpu.make_async_copy(tok_hbm, tok.at[k], load_sem.at[0]),
        pltpu.make_async_copy(wq_hbm, w.at[:, pl.ds(0, wide)], load_sem.at[1]),
        pltpu.make_async_copy(wv_hbm, w.at[:, pl.ds(wide, wide)], load_sem.at[2]),
        pltpu.make_async_copy(wo_hbm, wo, load_sem.at[3]),
        pltpu.make_async_copy(
            wo_hbm.at[:, pl.ds(pl.multiple_of(k * wide, HD), wide)], wo_own.at[k], load_sem.at[4]
        ),
    ]
    for load in loads:
        load.start()

    barrier = pltpu.get_barrier_semaphore()

    def greet(where):
        pl.semaphore_signal(barrier, inc=1, device_id=where, device_id_type=MESH)

    for m in range(1, n):
        greet({"head": lax.rem(k + m, n)})
    for m in range(1, ctx_count):
        greet({"ctx": lax.rem(ctx + m, ctx_count)})
    pl.semaphore_wait(barrier, n + ctx_count - 2)

    limit = jnp.where(doc == 0, lengths[0], lengths[1])

    def valid_rows(first, count):
        position = first + lax.broadcasted_iota(jnp.int32, (count, HD), 0)
        return jnp.where(position < limit, 1.0, 0.0)

    def chunk(c):
        return pl.ds(pl.multiple_of(c * step_rows, step_rows), step_rows)

    def tok_copy(source, c, to, sends):
        piece = tok.at[source, chunk(c)]
        return pltpu.make_async_remote_copy(
            src_ref=piece, dst_ref=piece, send_sem=sends.at[source, c],
            recv_sem=tok_recv.at[source, c], device_id={"head": to}, device_id_type=MESH,
        )

    def send_tok(source, c, up):
        if up:
            @pl.when(k < n - 1)
            def _():
                tok_copy(source, c, k + 1, up_send).start()
        else:
            @pl.when(k > 0)
            def _():
                tok_copy(source, c, k - 1, down_send).start()

    def arrive(source, c, up):
        tok_copy(source, c, k, up_send).wait_recv()
        send_tok(source, c, up)

    def kv_copy(slot, c, to, sem):
        piece = kv.at[slot, chunk(c)]
        return pltpu.make_async_remote_copy(
            src_ref=piece, dst_ref=piece, send_sem=sem, recv_sem=kv_recv.at[slot, c],
            device_id={"ctx": base + to}, device_id_type=MESH,
        )

    def behind(m):
        return lax.rem(j + g - 2 * m, g)

    def pass_on(c):
        for m in range(1, half):
            slot = behind(m)
            kv_copy(slot, c, partner, kv_pass.at[m, c]).wait_recv()
            kv_copy(slot, c, partner, kv_pass.at[m, c]).start()

    loads[0].wait()
    for c in range(AHEAD):
        send_tok(k, c, True)
        send_tok(k, c, False)
    ones[...] = jnp.concatenate(
        [valid_rows(block * rows, rows) for block in range(g)], axis=0
    ).astype(jnp.bfloat16)
    loads[1].wait()
    loads[2].wait()

    def gather_step(c, carry):
        def product(source):
            depth = pl.ds(pl.multiple_of(source * wide, HD), wide)
            return jnp.dot(tok[source, chunk(c)], w[depth], preferred_element_type=jnp.float32)

        projected[...] = product(k)
        for distance in range(1, n):
            @pl.when(k - distance >= 0)
            def _():
                arrive(k - distance, c, True)

            @pl.when(k + distance < n)
            def _():
                arrive(k + distance, c, False)

            @pl.when(k - distance >= 0)
            def _():
                projected[...] += product(k - distance)

            @pl.when(k + distance < n)
            def _():
                projected[...] += product(k + distance)

        @pl.when(c + AHEAD < gather_chunks)
        def _():
            send_tok(k, c + AHEAD, True)
            send_tok(k, c + AHEAD, False)

        total = projected[...]
        valid = valid_rows(j * rows + c * step_rows, step_rows)
        for h in range(heads):
            columns = slice(h * HD, (h + 1) * HD)
            part = total[:, columns]
            unit = part * lax.rsqrt(jnp.sum(part * part, axis=1, keepdims=True) + 1e-06)
            kv[j, chunk(c), columns] = unit.astype(jnp.bfloat16)
            q[chunk(c), columns] = (unit * EXP2_SCALE).astype(jnp.bfloat16)
            shifted = slice(wide + h * HD, wide + (h + 1) * HD)
            kv[j, chunk(c), shifted] = (total[:, shifted] * valid).astype(jnp.bfloat16)
        for m in range(1, half):
            kv_copy(j, c, lax.rem(j + 2 * m, g), kv_send.at[m, c]).start()
        kv_copy(j, c, partner, kv_send.at[0, c]).start()

        @pl.when(c > 0)
        def _():
            pass_on(c - 1)

        return carry

    lax.fori_loop(0, gather_chunks, gather_step, 0)
    loads[3].wait()
    loads[4].wait()

    def deal_copy(d):
        mine = pl.ds(pl.multiple_of(ctx * deal_rows, deal_rows), deal_rows)
        return pltpu.make_async_remote_copy(
            src_ref=wo.at[mine, pl.ds(pl.multiple_of(d * wide, HD), wide)],
            dst_ref=wo_own.at[k, mine], send_sem=deal_send.at[d], recv_sem=wo_recv.at[k, ctx],
            device_id={"head": d}, device_id_type=MESH,
        )

    def share_copy(source, dealer, to):
        piece = wo_own.at[
            source, pl.ds(pl.multiple_of(dealer * deal_rows, deal_rows), deal_rows)
        ]
        return pltpu.make_async_remote_copy(
            src_ref=piece, dst_ref=piece, send_sem=share_send.at[source, to],
            recv_sem=wo_recv.at[source, dealer], device_id={"ctx": to}, device_id_type=MESH,
        )

    def other(m):
        return lax.rem(ctx + m, ctx_count)

    for m in range(1, n):
        deal_copy(lax.rem(k + m, n)).start()

    def settle(slot):
        def landed(c, carry):
            kv_copy(slot, c, partner, kv_send.at[0, c]).wait_recv()
            return carry

        lax.fori_loop(0, gather_chunks, landed, 0)

    blocks = [j, partner]
    blocks += [behind(m) for m in range(1, half)]
    blocks += [lax.rem(partner + g - 2 * m, g) for m in range(1, half)]

    def sum_copy(c, d, to, landing, recv):
        return pltpu.make_async_remote_copy(
            src_ref=outgoing.at[c, d], dst_ref=landing.at[c, d], send_sem=sum_send.at[c, d],
            recv_sem=recv.at[c, d], device_id={"head": to}, device_id_type=MESH,
        )

    def query_chunk(c):
        return pl.ds(pl.multiple_of(c * query_rows, query_rows), query_rows)

    def share(d):
        columns = pl.ds(pl.multiple_of(d * wide, HD), wide)
        return jnp.dot(att[...], wo[:, columns], preferred_element_type=jnp.float32)

    def attend(c, target):
        own = c * query_rows
        valid = valid_rows(j * rows + own, query_rows)
        row = lax.broadcasted_iota(jnp.int32, (query_rows, rows), 0) + own
        column = lax.broadcasted_iota(jnp.int32, (query_rows, rows), 1)
        for b, block in enumerate(blocks):
            if b == 1 or b > half:
                @pl.when(c == 0)
                def _():
                    settle(block)
            if b == 2:
                @pl.when(c == 0)
                def _():
                    pass_on(gather_chunks - 1)

            block_rows = pl.ds(pl.multiple_of(block * rows, rows), rows)
            for h in range(heads):
                columns = slice(h * HD, (h + 1) * HD)
                shifted = slice(wide + h * HD, wide + (h + 1) * HD)
                scores = lax.dot_general(
                    q[query_chunk(c), columns], kv[block, :, columns],
                    (((1,), (1,)), ((), ())), preferred_element_type=jnp.float32,
                )
                weights = jnp.exp2(scores)
                if b == 0:
                    weights = jnp.where(row != column, weights, 0.0)
                values = jnp.concatenate(
                    [kv[block, :, shifted], ones[block_rows]], axis=1
                )
                term = jnp.dot(
                    weights.astype(jnp.bfloat16), values, preferred_element_type=jnp.float32
                )
                if b == 0:
                    mixed[h] = term
                else:
                    mixed[h] += term
        for h in range(heads):
            result = valid * mixed[h, :, :HD] / (mixed[h, :, HD:] + (1.0 - valid))
            target[:, h * HD:(h + 1) * HD] = result.astype(jnp.bfloat16)

    def emit(c, d, to, waits, landing, recv):
        @pl.when(waits)
        def _():
            sum_copy(c, d, k, landing, recv).wait_recv()
            outgoing[c, d] = (share(d) + landing[c, d].astype(jnp.float32)).astype(jnp.bfloat16)

        @pl.when(jnp.logical_not(waits))
        def _():
            outgoing[c, d] = share(d).astype(jnp.bfloat16)

        sum_copy(c, d, to, landing, recv).start()

    def spread_copy(c, s, to, sends):
        piece = spread.at[c, s]
        return pltpu.make_async_remote_copy(
            src_ref=piece, dst_ref=piece, send_sem=sends.at[c, s],
            recv_sem=spread_recv.at[c, s], device_id={"head": to}, device_id_type=MESH,
        )

    def relay(c, distance):
        @pl.when(jnp.logical_and(k - distance >= 0, k < n - 1))
        def _():
            spread_copy(c, k - distance, k, spread_up).wait_recv()
            spread_copy(c, k - distance, k + 1, spread_up).start()

        @pl.when(jnp.logical_and(k + distance < n, k > 0))
        def _():
            spread_copy(c, k + distance, k, spread_down).wait_recv()
            spread_copy(c, k + distance, k - 1, spread_down).start()

    def pair_step(c, carry):
        attend(2 * c, spread.at[c, k])

        @pl.when(k < n - 1)
        def _():
            spread_copy(c, k, k + 1, spread_up).start()

        @pl.when(k > 0)
        def _():
            spread_copy(c, k, k - 1, spread_down).start()

        @pl.when(c == 0)
        def _():
            for m in range(1, n):
                source = lax.rem(k + m, n)
                share_copy(source, ctx, ctx).wait_recv()

                def hand_out(step, inner):
                    share_copy(source, ctx, other(step)).start()
                    return inner

                lax.fori_loop(1, ctx_count, hand_out, 0)

        attend(2 * c + 1, att)
        relay(c, 1)
        for off in range(n - 1, 0, -1):
            @pl.when(k + off < n)
            def _():
                emit(c, k + off, k + 1, k > 0, from_low, low_recv)

            @pl.when(k - off >= 0)
            def _():
                emit(c, k - off, k - 1, k < n - 1, from_high, high_recv)

        own_sum[c] = share(k)
        for distance in range(2, n):
            relay(c, distance)
        return carry

    pairs = query_chunks // 2
    lax.fori_loop(0, pairs, pair_step, 0)

    def collect(step, carry):
        for m in range(1, n):
            share_copy(lax.rem(k + m, n), other(step), ctx).wait_recv()
        return carry

    lax.fori_loop(1, ctx_count, collect, 0)

    def finish(c, carry):
        for distance in range(1, n):
            @pl.when(jnp.logical_and(k - distance >= 0, k == n - 1))
            def _():
                spread_copy(c, k - distance, k, spread_up).wait_recv()

            @pl.when(jnp.logical_and(k + distance < n, k == 0))
            def _():
                spread_copy(c, k + distance, k, spread_down).wait_recv()

        total = jnp.dot(spread[c, 0], wo_own[0], preferred_element_type=jnp.float32)
        for s in range(1, n):
            total += jnp.dot(spread[c, s], wo_own[s], preferred_element_type=jnp.float32)
        out_ref[query_chunk(2 * c)] = total.astype(out_ref.dtype)

        @pl.when(k > 0)
        def _():
            sum_copy(c, k, k, from_low, low_recv).wait_recv()
            own_sum[c] += from_low[c, k].astype(jnp.float32)

        @pl.when(k < n - 1)
        def _():
            sum_copy(c, k, k, from_high, high_recv).wait_recv()
            own_sum[c] += from_high[c, k].astype(jnp.float32)

        out_ref[query_chunk(2 * c + 1)] = own_sum[c].astype(out_ref.dtype)
        return carry

    lax.fori_loop(0, pairs, finish, 0)

    def drain_gather(c, carry):
        for s in range(n):
            @pl.when(jnp.logical_and(s <= k, k < n - 1))
            def _():
                tok_copy(s, c, k + 1, up_send).wait_send()

            @pl.when(jnp.logical_and(s >= k, k > 0))
            def _():
                tok_copy(s, c, k - 1, down_send).wait_send()

        kv_copy(j, c, partner, kv_send.at[0, c]).wait_send()
        for m in range(1, half):
            kv_copy(j, c, partner, kv_send.at[m, c]).wait_send()
            kv_copy(behind(m), c, partner, kv_pass.at[m, c]).wait_send()
        return carry

    lax.fori_loop(0, gather_chunks, drain_gather, 0)

    def drain_sums(c, carry):
        for d in range(n):
            @pl.when(d > k)
            def _():
                sum_copy(c, d, k + 1, from_low, low_recv).wait_send()

            @pl.when(d < k)
            def _():
                sum_copy(c, d, k - 1, from_high, high_recv).wait_send()

            @pl.when(jnp.logical_and(d <= k, k < n - 1))
            def _():
                spread_copy(c, d, k + 1, spread_up).wait_send()

            @pl.when(jnp.logical_and(d >= k, k > 0))
            def _():
                spread_copy(c, d, k - 1, spread_down).wait_send()

        return carry

    lax.fori_loop(0, pairs, drain_sums, 0)
    for m in range(1, n):
        deal_copy(lax.rem(k + m, n)).wait_send()

    def drain_shares(step, carry):
        for m in range(1, n):
            share_copy(lax.rem(k + m, n), ctx, other(step)).wait_send()
        return carry

    lax.fori_loop(1, ctx_count, drain_shares, 0)


def per_device(tokens, w_query, w_value, w_out, doc_lengths):
    n = lax.axis_size("head")
    g = lax.axis_size("ctx") // 2
    rows, wide = tokens.shape
    depth = w_query.shape[0]
    query_rows = rows // QUERY_CHUNKS
    bf16, f32 = jnp.bfloat16, jnp.float32
    dma = pltpu.SemaphoreType.DMA
    any_space = pl.BlockSpec(memory_space=pl.ANY)
    pairs = QUERY_CHUNKS // 2
    pieces = (pairs, n, query_rows, wide)
    return pl.pallas_call(
        functools.partial(layer_kernel, n, g),
        out_shape=jax.ShapeDtypeStruct((rows, wide), bf16),
        in_specs=[any_space] * 4 + [pl.BlockSpec(memory_space=pltpu.SMEM)],
        out_specs=pl.BlockSpec(memory_space=pltpu.VMEM),
        scratch_shapes=[
            pltpu.VMEM((n, rows, wide), bf16),
            pltpu.VMEM((depth, 2 * wide), bf16),
            pltpu.VMEM(w_out.shape, bf16),
            pltpu.VMEM((rows, wide), bf16),
            pltpu.VMEM((g, rows, 2 * wide), bf16),
            pltpu.VMEM((g * rows, HD), bf16),
            pltpu.VMEM((query_rows, wide), bf16),
            pltpu.VMEM(pieces, bf16),
            pltpu.VMEM(pieces, bf16),
            pltpu.VMEM(pieces, bf16),
            pltpu.VMEM((pairs, query_rows, wide), f32),
            pltpu.VMEM(pieces, bf16),
            pltpu.VMEM((n, wide, wide), bf16),
            pltpu.VMEM((rows // GATHER_CHUNKS, 2 * wide), f32),
            pltpu.VMEM((wide // HD, query_rows, 2 * HD), f32),
            dma((5,)),
            dma((n, GATHER_CHUNKS)),
            dma((n, GATHER_CHUNKS)),
            dma((n, GATHER_CHUNKS)),
            dma((g // 2, GATHER_CHUNKS)),
            dma((g // 2, GATHER_CHUNKS)),
            dma((g, GATHER_CHUNKS)),
            dma((pairs, n)),
            dma((pairs, n)),
            dma((pairs, n)),
            dma((pairs, n)),
            dma((pairs, n)),
            dma((pairs, n)),
            dma((n,)),
            dma((n, 2 * g)),
            dma((n, 2 * g)),
        ],
        compiler_params=pltpu.CompilerParams(
            collective_id=0, has_side_effects=True, vmem_limit_bytes=60 * 1024 * 1024
        ),
    )(tokens, w_query, w_value, w_out, doc_lengths)


def solution(mesh):
    return jax.shard_map(
        per_device,
        mesh=mesh,
        in_specs=(P("ctx", "head"), P(None, "head"), P(None, "head"), P("head", None), P()),
        out_specs=P("ctx", "head"),
        check_vma=False,
    )
```
